256 devices in a mesh: row: 16 (over z_hi, y, core), col: 16 (over z_lo, x).
Axes of the slice: x: 4, y: 4, z: 8 (z_hi: 2, z_lo: 4; z = z_hi * 4 + z_lo), core: 2. Of those that a mesh axis runs over, the one named last changes fastest.
Arguments:
- features: bfloat16 [65536, 128], P(('col', 'row')), may hold values from -6 to 6
- weight: bfloat16 [128, 128], replicated, may hold values from -0.5 to 0.5
- tiles: bfloat16 [16, 16, 352, 128, 128], P('row', 'col'), may hold values from -0.0546875 to 0.0546875
- tile_slots: int32 [16, 16, 352], P('row', 'col'), may hold values from 0 to 1023, as said below
- tile_counts: int32 [16, 16], P('row', 'col'), may hold values from 44 to 352, as said below
- cotangent: bfloat16 [65536, 128], P(('row', 'col')), may hold values from -6 to 6
Outputs:
- hidden: bfloat16 [65536, 128], P(('row', 'col'))
- feature_grad: bfloat16 [65536, 128], P(('col', 'row'))
- weight_grad: float32 [128, 128], replicated
The draws below stay inside these ranges and needn't reach their ends.
Inputs may be any that keep to these rules, and one draw needn't show every extreme that they name: `tile_slots`: the slots of one block are distinct. `tile_counts`: some block has all 352 slots live.
All inputs are finite; a program needn't handle non-finite values.
Results may differ from the reference program's by a relative error of at most 0.006.
Values may be sent and summed in bfloat16 or wider, within the bound.
A program may use at most 128 MiB of HBM per device.

```python
import math
import jax
import jax.numpy as jnp
from jax import lax

FEAT = 128
TILE = 128
SHARE = 256
TROWS = 32
MAXT = 352
NODES = 65536
N_ROW = 16
N_COL = 16


def draw_tile_slots(key, part):
    tile_rows = SHARE * N_COL // TILE
    tile_cols = SHARE * N_ROW // TILE
    keys = jax.random.split(jax.random.fold_in(key, 11), N_ROW * N_COL)
    picked = jax.vmap(lambda sub: jax.random.permutation(sub, tile_rows * tile_cols)[:MAXT])(keys)
    return picked.astype(jnp.int32).reshape(N_ROW, N_COL, MAXT)


def draw_tile_counts(key, part):
    blocks = N_ROW * N_COL
    lowest = MAXT // 8
    raw = jax.random.randint(jax.random.fold_in(key, 21), (blocks,), 0, 64)
    counts = lowest + raw * raw * (MAXT - lowest) // (63 * 63)
    fullest = jax.random.randint(jax.random.fold_in(key, 22), (), 0, blocks)
    places = jnp.arange(blocks, dtype=jnp.int32)
    counts = jnp.where(places == fullest, MAXT, counts)
    counts = jnp.where(places == (fullest + 1) % blocks, lowest, counts)
    return counts.astype(jnp.int32).reshape(N_ROW, N_COL)


def steps_of(stream_key, shape, shards, least, largest):
    level = 1.0
    for axis_at, shards_of in shards:
        steps = jax.random.uniform(jax.random.fold_in(jax.random.fold_in(stream_key, 6), axis_at), (shards_of,), jnp.float32, least / len(shards), largest / len(shards))
        level = level * jnp.repeat(jnp.exp(steps), shape[axis_at] // shards_of).reshape((-1,) + (1,) * (len(shape) - 1 - axis_at))
    return level


def gaussian(own_key, extent, width, limit, cuts=(), kind=jnp.bfloat16):
    gain = steps_of(own_key, extent, cuts, -0.22, 0.18) if cuts else 1.0
    drawn = jax.random.normal(own_key, extent, jnp.float32) * width * gain
    return jnp.minimum(jnp.maximum(drawn, -limit), limit).astype(kind)


def setup_inputs(seed: int = 0) -> dict:
    splits = jax.random.split(jax.random.key(seed), 7)
    return {
        "features": gaussian(splits[0], (NODES, FEAT), 1.0, 6.0, ((0, 256),)),
        "weight": gaussian(splits[1], (FEAT, FEAT), FEAT ** -0.5, 0.5),
        "tiles": gaussian(splits[2], (N_ROW, N_COL, MAXT, TILE, TILE), (TILE * MAXT * N_COL // (2 * TROWS)) ** -0.5, 0.0546875, ((0, 16), (1, 16))),
        "tile_slots": draw_tile_slots(jax.random.fold_in(splits[6], 71), 0),
        "tile_counts": draw_tile_counts(jax.random.fold_in(splits[6], 71), 0),
        "cotangent": gaussian(splits[5], (NODES, FEAT), 1.0, 6.0, ((0, 256),)),
    }


def silu_grad(values):
    sig = jax.nn.sigmoid(values)
    return sig * (1.0 + values * (1.0 - sig))

def reference(features, weight, tiles, tile_slots, tile_counts, cotangent):
    tile_rows = SHARE * N_COL // TILE
    tile_cols = SHARE * N_ROW // TILE
    block_rows = SHARE * N_COL
    block_cols = SHARE * N_ROW
    projected = jnp.dot(features, weight, preferred_element_type=jnp.float32).astype(jnp.bfloat16)
    proj_blocks = projected.reshape(N_COL, block_cols, FEAT)
    live_mask = (jnp.arange(MAXT, dtype=jnp.int32)[None, None, :] < tile_counts[:, :, None]).astype(jnp.float32)

    def fwd_one(tile_vals, slot_ids, mask_row, proj_block):
        gathered = proj_block.reshape(tile_cols, TILE, FEAT)[slot_ids % tile_cols]
        products = jnp.einsum('tij,tjf->tif', tile_vals.astype(jnp.float32), gathered.astype(jnp.float32)) * mask_row[:, None, None]
        return jax.ops.segment_sum(products, slot_ids // tile_cols, tile_rows).reshape(block_rows, FEAT)

    def fwd_row(inputs):
        tile_vals, slot_ids, mask_rows = inputs
        return lax.optimization_barrier(jnp.sum(jax.vmap(fwd_one)(tile_vals, slot_ids, mask_rows, proj_blocks), axis=0))
    summed = lax.map(fwd_row, (tiles, tile_slots, live_mask)).reshape(NODES, FEAT)
    hidden = jax.nn.silu(summed).astype(jnp.bfloat16)
    grad_sum = (cotangent.astype(jnp.float32) * silu_grad(summed)).astype(jnp.bfloat16)
    grad_rows = grad_sum.reshape(N_ROW, block_rows, FEAT)

    def bwd_one(tile_vals, slot_ids, mask_row, grad_block):
        gathered = grad_block.reshape(tile_rows, TILE, FEAT)[slot_ids // tile_cols]
        products = jnp.einsum('tji,tjf->tif', tile_vals.astype(jnp.float32), gathered.astype(jnp.float32)) * mask_row[:, None, None]
        return jax.ops.segment_sum(products, slot_ids % tile_cols, tile_cols).reshape(block_cols, FEAT)

    def bwd_step(accum, inputs):
        tile_vals, slot_ids, mask_rows, grad_block = inputs
        terms = jax.vmap(bwd_one, in_axes=(0, 0, 0, None))(tile_vals, slot_ids, mask_rows, grad_block)
        return (accum + terms, None)
    start = jnp.zeros((N_COL, block_cols, FEAT), jnp.float32)
    accum, _ = lax.scan(bwd_step, start, (tiles, tile_slots, live_mask, grad_rows))
    grad_proj = accum.reshape(NODES, FEAT).astype(jnp.bfloat16)
    feature_grad = jnp.dot(grad_proj, weight.T, preferred_element_type=jnp.float32).astype(jnp.bfloat16)
    weight_grad = jnp.dot(features.T, grad_proj, preferred_element_type=jnp.float32) / math.sqrt(NODES)
    return (hidden, feature_grad, weight_grad)
```

```python
import functools
import math

import jax
import jax.numpy as jnp
from jax import lax
from jax.experimental import pallas as pl
from jax.experimental.pallas import tpu as pltpu
from jax.sharding import PartitionSpec as P

BF16 = jnp.bfloat16
F32 = jnp.float32

ROW_SPLIT = (2, 4, 2)
COL_SPLIT = (4, 4)


def layer_kernel(dims, smap, feat, wt, tiles, cot, hid, fg, wg, TV, FB, GB, GT, SX, RX, OX, SZ, RZ, SC, RC, SY, RY, OY, SH, RH,
                 W0, W1, WX, WZ, WC, WY, WH, WA, WB, tile_sem, a_send, a_recv, x_send, x_recv, z_send, z_recv, g_send, g_recv,
                 c_send, c_recv, y_send, y_recv, h_send, h_recv, w_send, w_recv):
    ZH, Y, C, ZL, X = dims
    R, Q = ZH * Y * C, ZL * X
    B, F = feat.shape
    T = tiles.shape[-1]
    S = tiles.shape[0]
    U = B // T
    NR, NC = Q * U, R * U
    r, q = lax.axis_index("row"), lax.axis_index("col")
    core, y, zh = r % C, (r // C) % Y, r // (C * Y)
    x, z = q % X, q // X
    rid = lambda h, b, c: (h * Y + b) * C + c
    cid = lambda a, b: a * X + b
    rows_of = lambda blk: pl.ds(pl.multiple_of(blk * B, B), B)
    sends = []

    def put(src, dst, ssem, rsem, **where):
        copy = pltpu.make_async_remote_copy(src_ref=src, dst_ref=dst, send_sem=ssem, recv_sem=rsem, device_id=where,
                                            device_id_type=pl.DeviceIdType.MESH)
        copy.start()
        sends.append(copy)

    def got(dst, ssem, rsem):
        pltpu.make_async_remote_copy(src_ref=dst, dst_ref=dst, send_sem=ssem, recv_sem=rsem, device_id={"row": r},
                                     device_id_type=pl.DeviceIdType.MESH).wait_recv()

    def sent(src, ssem, rsem):
        pltpu.make_async_remote_copy(src_ref=src, dst_ref=src, send_sem=ssem, recv_sem=rsem, device_id={"row": r},
                                     device_id_type=pl.DeviceIdType.MESH).wait_send()

    row_peers = ([rid((zh + d) % ZH, y, core) for d in range(1, ZH)] + [rid(zh, (y + d) % Y, core) for d in range(1, Y)]
                 + [rid(zh, y, (core + d) % C) for d in range(1, C)])
    col_peers = [cid((z + d) % ZL, x) for d in range(1, ZL)] + [cid(z, (x + d) % X) for d in range(1, X)]

    barrier = pltpu.get_barrier_semaphore()
    for p in row_peers:
        pl.semaphore_signal(barrier, inc=1, device_id={"row": p}, device_id_type=pl.DeviceIdType.MESH)
    for p in col_peers:
        pl.semaphore_signal(barrier, inc=1, device_id={"col": p}, device_id_type=pl.DeviceIdType.MESH)
    chunks = tile_sem.shape[0]
    loads = [pltpu.make_async_copy(tiles.at[pl.ds(i * (S // chunks), S // chunks)], TV.at[pl.ds(i * (S // chunks), S // chunks)],
                                   tile_sem.at[i]) for i in range(chunks)]
    for load in loads:
        load.start()
    TV[S] = jnp.zeros((T, T), BF16)
    FB[rows_of(r), :] = feat[...]
    pl.semaphore_wait(barrier, len(row_peers) + len(col_peers))

    n = 0

    def a_put(src, blk, dst_row):
        nonlocal n
        put(src, FB.at[rows_of(blk), :], a_send.at[n], a_recv.at[blk], row=dst_row)
        n += 1

    def a_got(blk):
        got(FB.at[rows_of(blk), :], a_send.at[0], a_recv.at[blk])

    for d in range(1, ZH):
        a_put(feat, r, rid((zh + d) % ZH, y, core))
    for d in range(1, Y):
        a_put(feat, r, rid(zh, (y + d) % Y, core))
    for d in range(1, C):
        a_put(feat, r, rid(zh, y, (core + d) % C))
    for d in range(1, Y):
        blk = rid(zh, (y + d) % Y, core)
        a_got(blk)
        for e in range(1, C):
            a_put(FB.at[rows_of(blk), :], blk, rid(zh, y, (core + e) % C))
    for h in range(1, ZH):
        blk = rid((zh + h) % ZH, y, core)
        a_got(blk)
        for d in range(1, Y):
            a_put(FB.at[rows_of(blk), :], blk, rid(zh, (y + d) % Y, core))
        for e in range(1, C):
            a_put(FB.at[rows_of(blk), :], blk, rid(zh, y, (core + e) % C))
    for h in range(1, ZH):
        for d in range(1, Y):
            blk = rid((zh + h) % ZH, (y + d) % Y, core)
            a_got(blk)
            for e in range(1, C):
                a_put(FB.at[rows_of(blk), :], blk, rid(zh, y, (core + e) % C))
    for e in range(1, C):
        for h in range(ZH):
            for d in range(Y):
                a_got(rid((zh + h) % ZH, (y + d) % Y, (core + e) % C))
    for load in loads:
        load.wait()

    G = 2 if ZL % 2 == 0 else 1

    def forward(xt, zp):
        parts = []
        for k in range(G):
            base = cid(zp * G + k, xt) * (U * NC)
            for u in range(U):
                parts.append(jnp.concatenate([TV[smap[base + (u * NC + c)]] for c in range(NC)], 1))
        return jnp.dot(jnp.concatenate(parts, 0), FB[...], preferred_element_type=F32)

    def far(i, carry):
        d = i // (ZL // G)
        zp = i % (ZL // G)
        xt = (x + 1 + d) % X
        out = forward(xt, zp).astype(BF16)
        for k in range(G):
            zt = zp * G + k
            SX[d, zt] = out[k * B:(k + 1) * B]
            pltpu.make_async_remote_copy(src_ref=SX.at[d, zt], dst_ref=RX.at[d, zt], send_sem=x_send.at[d, zt],
                                         recv_sem=x_recv.at[d, zt], device_id={"col": cid(z, xt)},
                                         device_id_type=pl.DeviceIdType.MESH).start()
        return carry

    def near(zp, carry):
        out = forward(x, zp)
        for k in range(G):
            OX[zp * G + k] = out[k * B:(k + 1) * B]
        return carry

    lax.fori_loop(0, (X - 1) * (ZL // G), far, 0)
    lax.fori_loop(0, ZL // G, near, 0)
    own = None
    for d in list(range(1, ZL)) + [0]:
        zt = (z + d) % ZL
        own = OX[zt]
        for e in range(X - 1):
            got(RX.at[e, zt], x_send.at[e, zt], x_recv.at[e, zt])
            own = own + RX[e, zt].astype(F32)
        if d:
            SZ[d - 1] = own.astype(BF16)
            put(SZ.at[d - 1], RZ.at[d - 1], z_send.at[d - 1], z_recv.at[d - 1], col=cid(zt, x))
    for d in range(1, ZL):
        got(RZ.at[d - 1], z_send.at[d - 1], z_recv.at[d - 1])
        own = own + RZ[d - 1].astype(F32)

    high = own.astype(BF16)
    low = (own - high.astype(F32)).astype(BF16)
    summed = jnp.dot(high, wt[...], preferred_element_type=F32) + jnp.dot(low, wt[...], preferred_element_type=F32)
    sig = jax.nn.sigmoid(summed)
    grad = (cot[...].astype(F32) * (sig * (1.0 + summed * (1.0 - sig)))).astype(BF16)
    GB[rows_of(q), :] = grad

    n_g = 0

    def g_put(blk, dst_col):
        nonlocal n_g
        put(GB.at[rows_of(blk), :], GB.at[rows_of(blk), :], g_send.at[n_g], g_recv.at[blk], col=dst_col)
        n_g += 1

    def g_got(blk):
        got(GB.at[rows_of(blk), :], g_send.at[0], g_recv.at[blk])

    def turn(blk):
        GT[:, rows_of(blk)] = GB[rows_of(blk), :].T

    for d in range(1, ZL):
        g_put(q, cid((z + d) % ZL, x))
    for d in range(1, X):
        g_put(q, cid(z, (x + d) % X))
    hid[...] = (summed * sig).astype(BF16)

    both = (((0,), (0,)), ((), ()))
    W0[...] = lax.dot_general(high, grad, both, preferred_element_type=F32) + lax.dot_general(low, grad, both, preferred_element_type=F32)
    px = F // X
    pz = px // ZL
    n_w = 0

    def w_put(src, dst, at, **where):
        nonlocal n_w
        put(src, dst, w_send.at[n_w], w_recv.at[at], **where)
        n_w += 1

    def w_got(dst, at):
        got(dst, w_send.at[0], w_recv.at[at])

    at_x, at_z = 0, X
    at_c = at_z + ZL
    at_y = at_c + C
    at_h = at_y + Y
    at_a = at_h + ZH
    at_b = at_a + ZL
    part = lambda i, size: pl.ds(pl.multiple_of(i * size, size), size)
    for d in range(1, X):
        xt = (x + d) % X
        w_put(W0.at[part(xt, px), :], WX.at[d], at_x + d, col=cid(z, xt))

    def w_step1():
        total = W0[part(x, px), :]
        for d in range(1, X):
            w_got(WX.at[d], at_x + d)
            total = total + WX[d]
        W1[...] = total
        for d in range(1, ZL):
            zt = (z + d) % ZL
            w_put(W1.at[part(zt, pz), :], WZ.at[d], at_z + d, col=cid(zt, x))

    def w_step2():
        total = W1[part(z, pz), :]
        for d in range(1, ZL):
            w_got(WZ.at[d], at_z + d)
            total = total + WZ[d]
        WC[core] = total
        for d in range(1, C):
            w_put(WC.at[core], WC.at[core], at_c + core, row=rid(zh, y, (core + d) % C))

    def w_step3():
        for d in range(1, C):
            w_got(WC.at[(core + d) % C], at_c + (core + d) % C)
        total = WC[0]
        for i in range(1, C):
            total = total + WC[i]
        WY[y] = total
        for d in range(1, Y):
            w_put(WY.at[y], WY.at[y], at_y + y, row=rid(zh, (y + d) % Y, core))

    def w_step4():
        for d in range(1, Y):
            w_got(WY.at[(y + d) % Y], at_y + (y + d) % Y)
        total = WY[0]
        for i in range(1, Y):
            total = total + WY[i]
        WH[zh] = total
        for d in range(1, ZH):
            w_put(WH.at[zh], WH.at[zh], at_h + zh, row=rid((zh + d) % ZH, y, core))

    def w_step5():
        for d in range(1, ZH):
            w_got(WH.at[(zh + d) % ZH], at_h + (zh + d) % ZH)
        total = WH[0]
        for i in range(1, ZH):
            total = total + WH[i]
        WA[part(z, pz), :] = total
        for d in range(1, ZL):
            w_put(WA.at[part(z, pz), :], WA.at[part(z, pz), :], at_a + z, col=cid((z + d) % ZL, x))

    def w_step6():
        for d in range(1, ZL):
            w_got(WA.at[part((z + d) % ZL, pz), :], at_a + (z + d) % ZL)
        WB[part(x, px), :] = WA[...]
        for d in range(1, X):
            w_put(WA, WB.at[part(x, px), :], at_b + x, col=cid(z, (x + d) % X))

    def w_step7():
        for d in range(1, X):
            w_got(WB.at[part((x + d) % X, px), :], at_b + (x + d) % X)
        wg[...] = WB[...] * (1.0 / math.sqrt(B * R * Q))

    turn(q)
    for d in range(1, ZL):
        blk = cid((z + d) % ZL, x)
        g_got(blk)
        for e in range(1, X):
            g_put(blk, cid(z, (x + e) % X))
        turn(blk)
    w_step1()
    for a in range(ZL):
        for e in range(1, X):
            blk = cid((z + a) % ZL, (x + e) % X)
            g_got(blk)
            turn(blk)
    w_step2()

    def backward(blk):
        base = blk * U
        w = jnp.concatenate([jnp.concatenate([TV[smap[t * NC + base + u]] for u in range(U)], 1) for t in range(NR)], 0)
        return jnp.dot(GT[...], w, preferred_element_type=F32)

    K = ZH * Y

    def other(i, carry):
        d, k = i // K, i % K
        ct = (core + 1 + d) % C
        SC[d, k] = backward(k * C + ct).astype(BF16)
        pltpu.make_async_remote_copy(src_ref=SC.at[d, k], dst_ref=RC.at[d, k], send_sem=c_send.at[d, k], recv_sem=c_recv.at[d, k],
                                     device_id={"row": rid(zh, y, ct)}, device_id_type=pl.DeviceIdType.MESH).start()
        return carry

    def joined(ht, yt):
        k = ht * Y + yt
        out = backward(rid(ht, yt, core))
        for d in range(C - 1):
            got(RC.at[d, k], c_send.at[d, k], c_recv.at[d, k])
            out = out + RC[d, k].astype(F32)
        return out

    def along(i, carry):
        d, ht = i // ZH, i % ZH
        yt = (y + 1 + d) % Y
        SY[d, ht] = joined(ht, yt).astype(BF16)
        pltpu.make_async_remote_copy(src_ref=SY.at[d, ht], dst_ref=RY.at[d, ht], send_sem=y_send.at[d, ht], recv_sem=y_recv.at[d, ht],
                                     device_id={"row": rid(zh, yt, core)}, device_id_type=pl.DeviceIdType.MESH).start()
        return carry

    def stay(i, carry):
        OY[i] = joined((zh + 1 + i) % ZH, y)
        return carry

    half = (C - 1) * K // 2
    lax.fori_loop(0, half, other, 0)
    w_step3()
    lax.fori_loop(half, (C - 1) * K, other, 0)
    w_step4()
    lax.fori_loop(0, (Y - 1) * ZH, along, 0)
    w_step5()
    lax.fori_loop(0, ZH, stay, 0)
    w_step6()
    for i in range(ZH):
        ht = (zh + 1 + i) % ZH
        own = OY[i]
        for d in range(Y - 1):
            got(RY.at[d, ht], y_send.at[d, ht], y_recv.at[d, ht])
            own = own + RY[d, ht].astype(F32)
        if i < ZH - 1:
            SH[i] = own.astype(BF16)
            put(SH.at[i], RH.at[i], h_send.at[i], h_recv.at[i], row=rid(ht, y, core))
    w_step7()
    for i in range(ZH - 1):
        got(RH.at[i], h_send.at[i], h_recv.at[i])
        own = own + RH[i].astype(F32)
    proj = own.astype(BF16).T
    fg[...] = lax.dot_general(proj, wt[...], (((1,), (1,)), ((), ())), preferred_element_type=F32).astype(BF16)

    for copy in sends:
        copy.wait_send()
    for d in range(X - 1):
        for k in range(ZL):
            sent(SX.at[d, k], x_send.at[d, k], x_recv.at[d, k])
    for d in range(C - 1):
        for k in range(K):
            sent(SC.at[d, k], c_send.at[d, k], c_recv.at[d, k])
    for d in range(Y - 1):
        for k in range(ZH):
            sent(SY.at[d, k], y_send.at[d, k], y_recv.at[d, k])


def body(dims, features, weight, tiles, tile_slots, tile_counts, cotangent):
    ZH, Y, C, ZL, X = dims
    R, Q = ZH * Y * C, ZL * X
    tile_vals, slot_ids, live_count = tiles[0, 0], tile_slots[0, 0], tile_counts[0, 0]
    S, T = tile_vals.shape[0], tile_vals.shape[-1]
    B, F = features.shape
    places = (B * Q // T) * (B * R // T)
    order = jnp.arange(S, dtype=jnp.int32)
    hit = (slot_ids[None, :] == jnp.arange(places, dtype=jnp.int32)[:, None]) & (order < live_count)[None, :]
    smap = S + jnp.sum(jnp.where(hit, order - S, 0), axis=1)
    dma = pltpu.SemaphoreType.DMA
    n1 = lambda v: max(v, 1)
    px = F // X
    pz = px // ZL
    blocks = lambda *lead: pltpu.VMEM((*lead, B, F), BF16)
    turned = lambda *lead: pltpu.VMEM((*lead, F, B), BF16)
    n_row = ZH * Y * C - 1
    n_w = 2 * (X - 1) + 2 * (ZL - 1) + (C - 1) + (Y - 1) + (ZH - 1)
    scratch = [
        pltpu.VMEM((S + 1, T, T), BF16),
        pltpu.VMEM((B * R, F), BF16),
        pltpu.VMEM((B * Q, F), BF16),
        pltpu.VMEM((F, B * Q), BF16),
        blocks(n1(X - 1), ZL), blocks(n1(X - 1), ZL),
        pltpu.VMEM((ZL, B, F), F32),
        blocks(n1(ZL - 1)), blocks(n1(ZL - 1)),
        turned(n1(C - 1), ZH * Y), turned(n1(C - 1), ZH * Y),
        turned(n1(Y - 1), ZH), turned(n1(Y - 1), ZH),
        pltpu.VMEM((ZH, F, B), F32),
        turned(n1(ZH - 1)), turned(n1(ZH - 1)),
        pltpu.VMEM((F, F), F32), pltpu.VMEM((px, F), F32),
        pltpu.VMEM((X, px, F), F32), pltpu.VMEM((ZL, pz, F), F32),
        pltpu.VMEM((C, pz, F), F32), pltpu.VMEM((Y, pz, F), F32), pltpu.VMEM((ZH, pz, F), F32),
        pltpu.VMEM((px, F), F32), pltpu.VMEM((F, F), F32),
        dma((8,)),
        dma((n_row,)), dma((R,)),
        dma((n1(X - 1), ZL)), dma((n1(X - 1), ZL)),
        dma((n1(ZL - 1),)), dma((n1(ZL - 1),)),
        dma((Q - 1,)), dma((Q,)),
        dma((n1(C - 1), ZH * Y)), dma((n1(C - 1), ZH * Y)),
        dma((n1(Y - 1), ZH)), dma((n1(Y - 1), ZH)),
        dma((n1(ZH - 1),)), dma((n1(ZH - 1),)),
        dma((n_w,)), dma((2 * X + 2 * ZL + C + Y + ZH,)),
    ]
    vmem = pl.BlockSpec(memory_space=pltpu.VMEM)
    return pl.pallas_call(
        functools.partial(layer_kernel, dims),
        name="graph_layer",
        out_shape=(jax.ShapeDtypeStruct((B, F), BF16), jax.ShapeDtypeStruct((B, F), BF16), jax.ShapeDtypeStruct((F, F), F32)),
        in_specs=[pl.BlockSpec(memory_space=pltpu.SMEM), vmem, vmem, pl.BlockSpec(memory_space=pl.ANY), vmem],
        out_specs=(vmem, vmem, vmem),
        scratch_shapes=scratch,
        compiler_params=pltpu.CompilerParams(collective_id=0, has_side_effects=True, vmem_limit_bytes=60 * 1024 * 1024),
    )(smap, features, weight, tile_vals, cotangent)


def solution(mesh, dims=ROW_SPLIT + COL_SPLIT):
    placed = (
        P(("col", "row"), None),
        P(),
        P("row", "col", None, None, None),
        P("row", "col", None),
        P("row", "col"),
        P(("row", "col"), None),
    )
    return jax.shard_map(
        functools.partial(body, dims),
        mesh=mesh,
        in_specs=placed,
        out_specs=(P(("row", "col"), None), P(("col", "row"), None), P()),
        check_vma=False,
    )
```

```python
import functools
import math

import jax
import jax.numpy as jnp
from jax import lax
from jax.experimental import pallas as pl
from jax.experimental.pallas import tpu as pltpu
from jax.sharding import PartitionSpec as P

BF16 = jnp.bfloat16
F32 = jnp.float32

ROW_SPLIT = (2, 4, 2)
COL_SPLIT = (4, 4)


def layer_kernel(dims, smap, feat, wt, tiles, cot, hid, fg, wg, TV, FB, GB, GT, AX, AR, S2, RP, RM, S1, R1, OX, SZ, RZ, SC, RC,
                 T2, QP, QM, T1, Q1, OY, SH, RH, W0, W1, WX, WZ, WC, WY, WH, WA, WB, tile_sem, a_send, a_recv, p_send, p_recv,
                 m_send, m_recv, x_send, x_recv, z_send, z_recv, g_send, g_recv, c_send, c_recv, u_send, u_recv, v_send, v_recv,
                 y_send, y_recv, h_send, h_recv, w_send, w_recv):
    ZH, Y, C, ZL, X = dims
    R, Q = ZH * Y * C, ZL * X
    B, F = feat.shape
    T = tiles.shape[-1]
    S = tiles.shape[0]
    U = B // T
    NC = R * U
    r, q = lax.axis_index("row"), lax.axis_index("col")
    core, y, zh = r % C, (r // C) % Y, r // (C * Y)
    x, z = q % X, q // X
    rid = lambda h, b, c: (h * Y + b) * C + c
    cid = lambda a, b: a * X + b
    span = lambda i, size: pl.ds(pl.multiple_of(i * size, size), size)
    rows_of = lambda blk: span(blk, B)
    half_of = lambda blk, k: span(blk * 2 + k, B // 2)
    xp, xm, x2 = (x + 1) % X, (x + X - 1) % X, (x + 2) % X
    yp, ym, y2 = (y + 1) % Y, (y + Y - 1) % Y, (y + 2) % Y
    z_near = {1: [], 2: [1 - z], 4: [z + 1 - 2 * (z % 2), (z + 2) % 4, 3 - z]}[ZL]
    h_peers = [(zh + d) % ZH for d in range(1, ZH)]
    c_peers = [(core + d) % C for d in range(1, C)]
    sends = []

    def put(src, dst, ssem, rsem, **where):
        copy = pltpu.make_async_remote_copy(src_ref=src, dst_ref=dst, send_sem=ssem, recv_sem=rsem, device_id=where,
                                            device_id_type=pl.DeviceIdType.MESH)
        copy.start()
        sends.append(copy)

    def got(dst, ssem, rsem):
        pltpu.make_async_remote_copy(src_ref=dst, dst_ref=dst, send_sem=ssem, recv_sem=rsem, device_id={"row": r},
                                     device_id_type=pl.DeviceIdType.MESH).wait_recv()

    row_peers = ([rid(h, y, core) for h in h_peers] + [rid(zh, (y + d) % Y, core) for d in range(1, Y)]
                 + [rid(zh, y, c) for c in c_peers])
    col_peers = [cid(a, x) for a in z_near] + [cid(z, (x + d) % X) for d in range(1, X)]

    barrier = pltpu.get_barrier_semaphore()
    for p in row_peers:
        pl.semaphore_signal(barrier, inc=1, device_id={"row": p}, device_id_type=pl.DeviceIdType.MESH)
    for p in col_peers:
        pl.semaphore_signal(barrier, inc=1, device_id={"col": p}, device_id_type=pl.DeviceIdType.MESH)
    chunks = tile_sem.shape[0]
    loads = [pltpu.make_async_copy(tiles.at[pl.ds(i * (S // chunks), S // chunks)], TV.at[pl.ds(i * (S // chunks), S // chunks)],
                                   tile_sem.at[i]) for i in range(chunks)]
    for load in loads:
        load.start()
    TV[S] = jnp.zeros((T, T), BF16)
    FB[rows_of(r), :] = feat[...]
    pl.semaphore_wait(barrier, len(row_peers) + len(col_peers))

    n_a = 0

    def a_put(at, blk, k, dst_row):
        nonlocal n_a
        put(FB.at[at, :], FB.at[at, :], a_send.at[n_a], a_recv.at[blk, k], row=dst_row)
        n_a += 1

    def a_got(at, blk, k):
        got(FB.at[at, :], a_send.at[0], a_recv.at[blk, k])

    def a_cores(blk):
        for c in c_peers:
            a_put(rows_of(blk), blk, 0, rid(zh, y, c))

    def a_ring(h):
        blk = rid(h, y, core)
        if Y > 1:
            a_put(rows_of(blk), blk, 0, rid(zh, yp, core))
            a_put(rows_of(blk), blk, 0, rid(zh, ym, core))
        a_cores(blk)

    def a_near(h):
        if Y > 1:
            left, right = rid(h, ym, core), rid(h, yp, core)
            a_got(rows_of(left), left, 0)
            a_put(half_of(left, 0), left, 0, rid(zh, yp, core))
            a_cores(left)
            a_got(rows_of(right), right, 0)
            a_put(half_of(right, 1), right, 1, rid(zh, ym, core))
            a_cores(right)

    def a_far(h):
        if Y > 1:
            blk = rid(h, y2, core)
            for k in range(2):
                a_got(half_of(blk, k), blk, k)
            a_cores(blk)

    def a_core(h):
        for c in c_peers:
            for b in range(Y):
                blk = rid(h, (y + b) % Y, c)
                a_got(rows_of(blk), blk, 0)

    for h in h_peers:
        a_put(rows_of(r), r, 0, rid(h, y, core))
    a_ring(zh)
    a_near(zh)
    a_far(zh)
    a_core(zh)
    for load in loads:
        load.wait()

    part_cols = NC // ZH

    def product(cids, h):
        parts = []
        for c in cids:
            for u in range(U):
                base = (c * U + u) * NC + h * part_cols
                parts.append(jnp.concatenate([TV[smap[base + t]] for t in range(part_cols)], 1))
        return jnp.dot(jnp.concatenate(parts, 0), FB[span(h, part_cols * T), :], preferred_element_type=F32)

    G = 2
    hs = [zh] + h_peers
    for at, h in enumerate(hs[:-1]):
        later = hs[at + 1]

        def collect(i, carry, at=at, h=h):
            out = product([i * G + k for k in range(G)], h)
            for k in range(G):
                blk = i * G + k
                AX[blk] = out[k * B:(k + 1) * B] if at == 0 else AX[blk] + out[k * B:(k + 1) * B]
            return carry

        stop = Q // G
        cuts = [0, stop * 3 // 8, stop * 6 // 8, stop]
        lax.fori_loop(cuts[0], cuts[1], collect, 0)
        blk = rid(later, y, core)
        a_got(rows_of(blk), blk, 0)
        a_ring(later)
        lax.fori_loop(cuts[1], cuts[2], collect, 0)
        a_near(later)
        lax.fori_loop(cuts[2], cuts[3], collect, 0)
        a_far(later)
        a_core(later)

    def forward(cids):
        out = product(cids, hs[-1])
        outs = [out[k * B:(k + 1) * B] for k in range(len(cids))]
        return [AX[c] + o for c, o in zip(cids, outs)] if ZH > 1 else outs

    zs = z_near[::-1] + [z]
    H = B // 2
    pairs = [tuple(range(i, min(i + G, ZL))) for i in range(0, ZL, G)]
    if X > 1:
        for pair in pairs:
            for i, out in zip(pair, forward([cid(zs[i], x2) for i in pair])):
                S2[i] = out.astype(BF16)
                put(S2.at[i, pl.ds(0, H)], RP.at[i], p_send.at[i], p_recv.at[i], col=cid(z, xp))
                put(S2.at[i, pl.ds(H, H)], RM.at[i], m_send.at[i], m_recv.at[i], col=cid(z, xm))

    def reduced(i):
        total = OX[i]
        if X > 1:
            for k in range(2):
                got(R1.at[k, i], x_send.at[k, i], x_recv.at[k, i])
                total = total + R1[k, i].astype(F32)
        if i < ZL - 1:
            SZ[i] = total.astype(BF16)
            put(SZ.at[i], RZ.at[i], z_send.at[i], z_recv.at[i], col=cid(zs[i], x))
        return total

    own = None
    for pair in pairs:
        for i, out in zip(pair, forward([cid(zs[i], x) for i in pair])):
            OX[i] = out
        for i in pair:
            if X > 1:
                plus, minus = forward([cid(zs[i], xp), cid(zs[i], xm)])
                got(RP.at[i], p_send.at[i], p_recv.at[i])
                S1[0, i, pl.ds(0, H)] = (plus[:H] + RP[i].astype(F32)).astype(BF16)
                S1[0, i, pl.ds(H, H)] = plus[H:].astype(BF16)
                put(S1.at[0, i], R1.at[0, i], x_send.at[0, i], x_recv.at[0, i], col=cid(z, xp))
                got(RM.at[i], m_send.at[i], m_recv.at[i])
                S1[1, i, pl.ds(0, H)] = minus[:H].astype(BF16)
                S1[1, i, pl.ds(H, H)] = (minus[H:] + RM[i].astype(F32)).astype(BF16)
                put(S1.at[1, i], R1.at[1, i], x_send.at[1, i], x_recv.at[1, i], col=cid(z, xm))
            if i >= 2:
                own = reduced(i - 2)
    for i in range(max(ZL - 2, 0), ZL):
        own = reduced(i)
    for i in range(ZL - 1):
        got(RZ.at[i], z_send.at[i], z_recv.at[i])
        own = own + RZ[i].astype(F32)

    high = own.astype(BF16)
    low = (own - high.astype(F32)).astype(BF16)
    summed = jnp.dot(high, wt[...], preferred_element_type=F32) + jnp.dot(low, wt[...], preferred_element_type=F32)
    sig = jax.nn.sigmoid(summed)
    grad = (cot[...].astype(F32) * (sig * (1.0 + summed * (1.0 - sig)))).astype(BF16)
    GB[rows_of(q), :] = grad

    n_g = 0

    def g_put(at, blk, k, dst_col):
        nonlocal n_g
        put(GB.at[at, :], GB.at[at, :], g_send.at[n_g], g_recv.at[blk, k], col=dst_col)
        n_g += 1

    def g_got(at, blk, k):
        got(GB.at[at, :], g_send.at[0], g_recv.at[blk, k])

    def turn(blk):
        GT[:, rows_of(blk)] = GB[rows_of(blk), :].T

    def g_ring(a):
        if X > 1:
            blk = cid(a, x)
            g_put(rows_of(blk), blk, 0, cid(z, xp))
            g_put(rows_of(blk), blk, 0, cid(z, xm))

    def g_take(a):
        blk = cid(a, x)
        g_got(rows_of(blk), blk, 0)
        g_ring(a)

    def g_near(a):
        turn(cid(a, x))
        if X > 1:
            left, right = cid(a, xm), cid(a, xp)
            g_got(rows_of(left), left, 0)
            g_put(half_of(left, 0), left, 0, cid(z, xp))
            g_got(rows_of(right), right, 0)
            g_put(half_of(right, 1), right, 1, cid(z, xm))
            turn(left)
            turn(right)

    def g_far(a):
        if X > 1:
            blk = cid(a, x2)
            for k in range(2):
                g_got(half_of(blk, k), blk, k)
            turn(blk)

    g_ring(z)
    for a in z_near:
        g_put(rows_of(q), q, 0, cid(a, x))
    hid[...] = (summed * sig).astype(BF16)

    both = (((0,), (0,)), ((), ()))
    W0[...] = lax.dot_general(high, grad, both, preferred_element_type=F32) + lax.dot_general(low, grad, both, preferred_element_type=F32)
    px = F // X
    pz = px // ZL
    n_w = 0

    def w_put(src, dst, at, **where):
        nonlocal n_w
        put(src, dst, w_send.at[n_w], w_recv.at[at], **where)
        n_w += 1

    def w_got(dst, at):
        got(dst, w_send.at[0], w_recv.at[at])

    at_x, at_z = 0, X
    at_c = at_z + ZL
    at_y = at_c + C
    at_h = at_y + Y
    at_a = at_h + ZH
    at_b = at_a + ZL
    for d in range(1, X):
        xt = (x + d) % X
        w_put(W0.at[span(xt, px), :], WX.at[d], at_x + d, col=cid(z, xt))

    def w_step1():
        total = W0[span(x, px), :]
        for d in range(1, X):
            w_got(WX.at[d], at_x + d)
            total = total + WX[d]
        W1[...] = total
        for d in range(1, ZL):
            zt = (z + d) % ZL
            w_put(W1.at[span(zt, pz), :], WZ.at[d], at_z + d, col=cid(zt, x))

    def w_step2():
        total = W1[span(z, pz), :]
        for d in range(1, ZL):
            w_got(WZ.at[d], at_z + d)
            total = total + WZ[d]
        WC[core] = total
        for d in range(1, C):
            w_put(WC.at[core], WC.at[core], at_c + core, row=rid(zh, y, (core + d) % C))

    def w_step3():
        for d in range(1, C):
            w_got(WC.at[(core + d) % C], at_c + (core + d) % C)
        total = WC[0]
        for i in range(1, C):
            total = total + WC[i]
        WY[y] = total
        for d in range(1, Y):
            w_put(WY.at[y], WY.at[y], at_y + y, row=rid(zh, (y + d) % Y, core))

    def w_step4():
        for d in range(1, Y):
            w_got(WY.at[(y + d) % Y], at_y + (y + d) % Y)
        total = WY[0]
        for i in range(1, Y):
            total = total + WY[i]
        WH[zh] = total
        for d in range(1, ZH):
            w_put(WH.at[zh], WH.at[zh], at_h + zh, row=rid((zh + d) % ZH, y, core))

    def w_step5():
        for d in range(1, ZH):
            w_got(WH.at[(zh + d) % ZH], at_h + (zh + d) % ZH)
        total = WH[0]
        for i in range(1, ZH):
            total = total + WH[i]
        WA[span(z, pz), :] = total
        for d in range(1, ZL):
            w_put(WA.at[span(z, pz), :], WA.at[span(z, pz), :], at_a + z, col=cid((z + d) % ZL, x))

    def w_step6():
        for d in range(1, ZL):
            w_got(WA.at[span((z + d) % ZL, pz), :], at_a + (z + d) % ZL)
        WB[span(x, px), :] = WA[...]
        for d in range(1, X):
            w_put(WA, WB.at[span(x, px), :], at_b + x, col=cid(z, (x + d) % X))

    def w_step7():
        for d in range(1, X):
            w_got(WB.at[span((x + d) % X, px), :], at_b + (x + d) % X)
        wg[...] = WB[...] * (1.0 / math.sqrt(B * R * Q))

    chunk = X * U

    def back(blk, a):
        w = jnp.concatenate([jnp.concatenate([TV[smap[(a * chunk + t) * NC + blk * U + u]] for u in range(U)], 1)
                             for t in range(chunk)], 0)
        return jnp.dot(GT[:, span(a, chunk * T)], w, preferred_element_type=F32)

    order = [z] + z_near

    def gather_back(at, lo, hi):
        def step(blk, carry):
            out = back(blk, order[at])
            AR[blk] = out if at == 0 else AR[blk] + out
            return carry

        lax.fori_loop(lo, hi, step, 0)

    for a in z_near[:1]:
        g_take(a)
    g_near(z)
    w_step1()
    for a in z_near[1:]:
        g_take(a)
    later = [w_step2, w_step3, w_step4]
    if ZL > 1:
        g_near(order[1])
    g_far(z)
    for at in range(ZL - 1):
        gather_back(at, 0, R // 2)
        if at + 2 < ZL:
            g_near(order[at + 2])
        if later:
            later.pop(0)()
        gather_back(at, R // 2, R)
        g_far(order[at + 1])
    for step in later:
        step()

    def last(blk):
        out = back(blk, order[-1])
        return AR[blk] + out if ZL > 1 else out

    E = F // 2
    places = [(i, j, h, b) for i, h in enumerate(h_peers + [zh]) for j, b in enumerate([y2, yp, ym, y] if Y > 1 else [y])]
    for d, c in enumerate(c_peers):
        for k, (i, j, h, b) in enumerate(places):
            SC[d, k] = last(rid(h, b, c)).astype(BF16)
            put(SC.at[d, k], RC.at[d, k], c_send.at[d, k], c_recv.at[d, k], row=rid(zh, y, c))
    w_step5()

    def settled(i):
        total = OY[i]
        if Y > 1:
            for k in range(2):
                got(Q1.at[k, i], y_send.at[k, i], y_recv.at[k, i])
                total = total + Q1[k, i].astype(F32)
        if i < ZH - 1:
            SH[i] = total.astype(BF16)
            put(SH.at[i], RH.at[i], h_send.at[i], h_recv.at[i], row=rid(h_peers[i], y, core))
        return total

    for k, (i, j, h, b) in enumerate(places):
        out = last(rid(h, b, core))
        for d in range(C - 1):
            got(RC.at[d, k], c_send.at[d, k], c_recv.at[d, k])
            out = out + RC[d, k].astype(F32)
        if Y == 1 or j == 3:
            OY[i] = out
        elif j == 0:
            T2[i] = out.astype(BF16)
            put(T2.at[i, pl.ds(0, E)], QP.at[i], u_send.at[i], u_recv.at[i], row=rid(zh, yp, core))
            put(T2.at[i, pl.ds(E, E)], QM.at[i], v_send.at[i], v_recv.at[i], row=rid(zh, ym, core))
        elif j == 1:
            got(QP.at[i], u_send.at[i], u_recv.at[i])
            T1[0, i, pl.ds(0, E)] = (out[:E] + QP[i].astype(F32)).astype(BF16)
            T1[0, i, pl.ds(E, E)] = out[E:].astype(BF16)
            put(T1.at[0, i], Q1.at[0, i], y_send.at[0, i], y_recv.at[0, i], row=rid(zh, yp, core))
        else:
            got(QM.at[i], v_send.at[i], v_recv.at[i])
            T1[1, i, pl.ds(0, E)] = out[:E].astype(BF16)
            T1[1, i, pl.ds(E, E)] = (out[E:] + QM[i].astype(F32)).astype(BF16)
            put(T1.at[1, i], Q1.at[1, i], y_send.at[1, i], y_recv.at[1, i], row=rid(zh, ym, core))
    own = settled(0)
    w_step6()
    for i in range(1, ZH):
        own = settled(i)
    w_step7()
    for i in range(ZH - 1):
        got(RH.at[i], h_send.at[i], h_recv.at[i])
        own = own + RH[i].astype(F32)
    proj = own.astype(BF16).T
    fg[...] = lax.dot_general(proj, wt[...], (((1,), (1,)), ((), ())), preferred_element_type=F32).astype(BF16)

    for copy in sends:
        copy.wait_send()


def place_kernel(a, b, c, oa, ob, oc):
    oa[...] = a[...]
    ob[...] = b[...]
    oc[...] = c[...]


def body(dims, features, weight, tiles, tile_slots, tile_counts, cotangent):
    ZH, Y, C, ZL, X = dims
    R, Q = ZH * Y * C, ZL * X
    tile_vals, slot_ids, live_count = tiles[0, 0], tile_slots[0, 0], tile_counts[0, 0]
    S, T = tile_vals.shape[0], tile_vals.shape[-1]
    B, F = features.shape
    places = (B * Q // T) * (B * R // T)
    order = jnp.arange(S, dtype=jnp.int32)
    hit = (slot_ids[None, :] == jnp.arange(places, dtype=jnp.int32)[:, None]) & (order < live_count)[None, :]
    smap = S + jnp.sum(jnp.where(hit, order - S, 0), axis=1)
    dma = pltpu.SemaphoreType.DMA
    n1 = lambda v: max(v, 1)
    px = F // X
    pz = px // ZL
    blocks = lambda *lead: pltpu.VMEM((*lead, B, F), BF16)
    turned = lambda *lead: pltpu.VMEM((*lead, F, B), BF16)
    half = lambda n: pltpu.VMEM((n, B // 2, F), BF16)
    thin = lambda n: pltpu.VMEM((n, F // 2, B), BF16)
    n_a = R * 2 + 8
    n_g = Q * 2 + 8
    n_w = 2 * (X - 1) + 2 * (ZL - 1) + (C - 1) + (Y - 1) + (ZH - 1)
    scratch = [
        pltpu.VMEM((S + 1, T, T), BF16),
        pltpu.VMEM((B * R, F), BF16),
        pltpu.VMEM((B * Q, F), BF16),
        pltpu.VMEM((F, B * Q), BF16),
        pltpu.VMEM((Q, B, F), F32), pltpu.VMEM((R, F, B), F32),
        blocks(ZL), half(ZL), half(ZL),
        blocks(2, ZL), blocks(2, ZL),
        pltpu.VMEM((ZL, B, F), F32),
        blocks(n1(ZL - 1)), blocks(n1(ZL - 1)),
        turned(n1(C - 1), ZH * Y), turned(n1(C - 1), ZH * Y),
        turned(ZH), thin(ZH), thin(ZH),
        turned(2, ZH), turned(2, ZH),
        pltpu.VMEM((ZH, F, B), F32),
        turned(n1(ZH - 1)), turned(n1(ZH - 1)),
        pltpu.VMEM((F, F), F32), pltpu.VMEM((px, F), F32),
        pltpu.VMEM((X, px, F), F32), pltpu.VMEM((ZL, pz, F), F32),
        pltpu.VMEM((C, pz, F), F32), pltpu.VMEM((Y, pz, F), F32), pltpu.VMEM((ZH, pz, F), F32),
        pltpu.VMEM((px, F), F32), pltpu.VMEM((F, F), F32),
        dma((8,)),
        dma((n_a,)), dma((R, 2)),
        dma((ZL,)), dma((ZL,)), dma((ZL,)), dma((ZL,)),
        dma((2, ZL)), dma((2, ZL)),
        dma((n1(ZL - 1),)), dma((n1(ZL - 1),)),
        dma((n_g,)), dma((Q, 2)),
        dma((n1(C - 1), ZH * Y)), dma((n1(C - 1), ZH * Y)),
        dma((ZH,)), dma((ZH,)), dma((ZH,)), dma((ZH,)),
        dma((2, ZH)), dma((2, ZH)),
        dma((n1(ZH - 1),)), dma((n1(ZH - 1),)),
        dma((n_w,)), dma((2 * X + 2 * ZL + C + Y + ZH,)),
    ]
    vmem = pl.BlockSpec(memory_space=pltpu.VMEM)
    outs = (jax.ShapeDtypeStruct((B, F), BF16), jax.ShapeDtypeStruct((B, F), BF16), jax.ShapeDtypeStruct((F, F), F32))
    found = pl.pallas_call(
        functools.partial(layer_kernel, dims),
        name="graph_layer",
        out_shape=outs,
        in_specs=[pl.BlockSpec(memory_space=pltpu.SMEM), vmem, vmem, pl.BlockSpec(memory_space=pl.ANY), vmem],
        out_specs=(vmem, vmem, vmem),
        scratch_shapes=scratch,
        compiler_params=pltpu.CompilerParams(collective_id=0, has_side_effects=True, vmem_limit_bytes=60 * 1024 * 1024),
    )(smap, features, weight, tile_vals, cotangent)
    return pl.pallas_call(place_kernel, name="place_outputs", out_shape=outs, in_specs=[vmem] * 3, out_specs=(vmem,) * 3)(*found)


def solution(mesh, dims=ROW_SPLIT + COL_SPLIT):
    placed = (
        P(("col", "row"), None),
        P(),
        P("row", "col", None, None, None),
        P("row", "col", None),
        P("row", "col"),
        P(("row", "col"), None),
    )
    return jax.shard_map(
        functools.partial(body, dims),
        mesh=mesh,
        in_specs=placed,
        out_specs=(P(("row", "col"), None), P(("col", "row"), None), P()),
        check_vma=False,
    )
```
